128 devices in a mesh: tm: 8 (over y_lo, x), space: 16 (over y_hi, z, core).
Axes of the slice: x: 4, y: 4 (y_hi: 2, y_lo: 2; y = y_hi * 2 + y_lo), z: 4, core: 2. Of those that a mesh axis runs over, the one named last changes fastest.
Arguments:
- frames_in: bfloat16 [32, 64, 64, 512], P('tm', 'space'), may hold values from -6 to 6
- spatial_kernel: bfloat16 [3, 3, 512, 512], replicated, may hold values from -0.09375 to 0.09375
- temporal_kernel: bfloat16 [3, 512, 512], replicated, may hold values from -0.15625 to 0.15625
- norm_gain: float32 [512], replicated, may hold values from 0.1 to 1.9
- query_weight: bfloat16 [512, 512], replicated, may hold values from -2 to 2
- key_weight: bfloat16 [512, 512], replicated, may hold values from -2 to 2
- value_weight: bfloat16 [512, 512], replicated, may hold values from -0.25 to 0.25
- out_weight: bfloat16 [512, 512], replicated, may hold values from -0.25 to 0.25
- cotangent: bfloat16 [32, 64, 64, 512], P('tm', 'space'), may hold values from -6 to 6
Outputs:
- encoded: bfloat16 [32, 64, 64, 512], P('tm', 'space')
- kernel_grad: float32 [3, 512, 512], P(None, 'tm', 'space')
The draws below stay inside these ranges and needn't reach their ends.
All inputs are finite; a program needn't handle non-finite values.
Results may differ from the reference program's by a relative error of at most 0.007.
Values may be sent and summed in bfloat16 or wider, within the bound.
A program may use at most 128 MiB of HBM per device.

```python
import jax
import jax.numpy as jnp
from jax import lax

C = 512
WCOL = 64
FRAMES = 32
ROWS = 64


def pair_weights(key):
    base = jax.random.normal(jax.random.fold_in(key, 11), (C, C), jnp.float32) * C ** (-0.5)
    other = jax.random.normal(jax.random.fold_in(key, 12), (C, C), jnp.float32) * C ** (-0.5)
    query = other
    return (jnp.clip(query, -2.0, 2.0), jnp.clip(base, -2.0, 2.0))


def draw_query_weight(key, part):
    return pair_weights(key)[0].astype(jnp.bfloat16)


def draw_key_weight(key, part):
    return pair_weights(key)[1].astype(jnp.bfloat16)


def draw_frames_in(key, part):
    values = jax.random.normal(jax.random.fold_in(key, 24), (FRAMES, ROWS, WCOL, C), jnp.float32)
    return jnp.clip(values, -6.0, 6.0).astype(jnp.bfloat16)


def spiked(drawn, rng, source, target, parts, factor):
    owner, partner = [(jnp.arange(drawn.shape[axis_at]) // (drawn.shape[axis_at] // parts)).reshape([-1 if axis == axis_at else 1 for axis in range(drawn.ndim)]) for axis_at in (source, target)]
    chosen = jax.random.permutation(rng, parts)[partner]
    strong = (owner == chosen) | (owner == (partner + parts // 2) % parts)
    return jnp.where(strong, factor * drawn, drawn)


def level_of(key, extent, cuts, low, high):
    def one(axis_at, parts):
        draws = jax.random.uniform(jax.random.fold_in(jax.random.fold_in(key, 6), axis_at), (parts,), jnp.float32, low / len(cuts), high / len(cuts))
        return jnp.repeat(jnp.exp(draws), extent[axis_at] // parts).reshape((-1,) + (1,) * (len(extent) - axis_at - 1))

    level = one(*cuts[0])
    for cut in cuts[1:]:
        level = level * one(*cut)
    return level


def centred(stream_key, shape, width, most, split=(), dtype=jnp.bfloat16):
    loudness = level_of(stream_key, shape, split, -0.22, 0.18) if split else 1.0
    drawn = jax.random.normal(stream_key, shape, jnp.float32) * width * loudness
    return jnp.minimum(jnp.maximum(drawn, -most), most).astype(dtype)


def bell_draw_with(own_key, shape, spread, limit, split, heavy, kind=jnp.bfloat16):
    values = spread * jax.random.normal(own_key, shape, jnp.float32)
    if split:
        values = values * level_of(own_key, shape, split, -0.22, 0.18)
    return jnp.clip(spiked(values, jax.random.fold_in(own_key, 3), *heavy), -limit, limit).astype(kind)


def setup_inputs(seed: int = 0) -> dict:
    keys = jax.random.split(jax.random.key(seed), 10)
    frames_in = draw_frames_in(jax.random.fold_in(keys[9], 71), 0)
    spatial_kernel = centred(keys[1], (3, 3, C, C), (9 * C) ** -0.5, 0.09375)
    temporal_kernel = centred(keys[2], (3, C, C), (3 * C) ** -0.5, 0.15625)
    norm_gain = jnp.clip(1.0 + 0.18 * jax.random.normal(keys[3], (C,), jnp.float32), 0.1, 1.9)
    query_weight = draw_query_weight(jax.random.fold_in(keys[9], 71), 0)
    key_weight = draw_key_weight(jax.random.fold_in(keys[9], 71), 0)
    value_weight = centred(keys[6], (C, C), C ** -0.5, 0.25)
    out_weight = centred(keys[7], (C, C), C ** -0.5, 0.25)
    cotangent = bell_draw_with(keys[8], (FRAMES, ROWS, WCOL, C), 1.0, 6.0, ((0, 8), (1, 16)), (1, 3, 16, 2.0))
    return dict(frames_in=frames_in, spatial_kernel=spatial_kernel, temporal_kernel=temporal_kernel, norm_gain=norm_gain, query_weight=query_weight, key_weight=key_weight, value_weight=value_weight, out_weight=out_weight, cotangent=cotangent)


def causal_attend(query, key, value):
    frames = query.shape[0]
    scores = jnp.einsum('anc,bnc->abn', query.astype(jnp.float32), key.astype(jnp.float32)) / jnp.sqrt(jnp.float32(query.shape[2]))
    rows = jnp.arange(frames)[:, None, None]
    cols = jnp.arange(frames)[None, :, None]
    allowed = cols <= rows
    scores = jnp.where(allowed, scores, jnp.float32(-1e+30))
    top = lax.optimization_barrier(jnp.max(scores, axis=1, keepdims=True))
    expon = jnp.where(allowed, jnp.exp(scores - top), jnp.float32(0.0))
    total = lax.optimization_barrier(jnp.sum(expon, axis=1))
    mixed = jnp.einsum('abn,bnc->anc', expon, value.astype(jnp.float32))
    return mixed / total[:, :, None]

def reference(frames_in, spatial_kernel, temporal_kernel, norm_gain, query_weight, key_weight, value_weight, out_weight, cotangent):
    frames, rows, cols, chans = frames_in.shape
    padded = jnp.pad(frames_in, ((0, 0), (1, 1), (1, 1), (0, 0)))
    spatial = jnp.zeros((frames * rows * cols, chans), jnp.float32)
    for di in range(3):
        for dj in range(3):
            piece = padded[:, di:di + rows, dj:dj + cols, :].reshape(-1, chans)
            spatial = spatial + jnp.dot(piece, spatial_kernel[di, dj], preferred_element_type=jnp.float32)
    act = jax.nn.silu(spatial).astype(jnp.bfloat16).reshape(frames, rows, cols, chans)
    extended = jnp.pad(act, ((2, 0), (0, 0), (0, 0), (0, 0)))
    temporal = jnp.zeros((frames * rows * cols, chans), jnp.float32)
    flat_grad = cotangent.reshape(-1, chans)
    grads = []
    for tap in range(3):
        shifted = extended[2 - tap:2 - tap + frames].reshape(-1, chans)
        temporal = temporal + jnp.dot(shifted, temporal_kernel[tap], preferred_element_type=jnp.float32)
        grads.append(jnp.einsum('nc,nd->cd', shifted, flat_grad, preferred_element_type=jnp.float32))
    hidden = (frames_in.reshape(-1, chans).astype(jnp.float32) + temporal).astype(jnp.bfloat16)
    wide = hidden.astype(jnp.float32)
    normed = (wide / jnp.sqrt(lax.optimization_barrier(jnp.mean(wide * wide, axis=1, keepdims=True)) + 1e-06) * norm_gain).astype(jnp.bfloat16)
    query = jnp.dot(normed, query_weight, preferred_element_type=jnp.float32).astype(jnp.bfloat16).reshape(frames, rows * cols, chans)
    key = jnp.dot(normed, key_weight, preferred_element_type=jnp.float32).astype(jnp.bfloat16).reshape(frames, rows * cols, chans)
    value = jnp.dot(normed, value_weight, preferred_element_type=jnp.float32).astype(jnp.bfloat16).reshape(frames, rows * cols, chans)
    attended = causal_attend(query, key, value).astype(jnp.bfloat16).reshape(-1, chans)
    encoded = (wide + jnp.dot(attended, out_weight, preferred_element_type=jnp.float32)).astype(jnp.bfloat16)
    return (encoded.reshape(frames, rows, cols, chans), jnp.stack(grads, axis=0))
```

```python
import jax
import jax.numpy as jnp
from jax import lax
from jax.sharding import PartitionSpec as P


def extended_2(cells, sides, width):
    for axis, dim in sides:
        count = lax.axis_size(axis)
        ends = count - 1
        head = lax.slice_in_dim(cells, 0, width, axis=dim)
        tail = lax.slice_in_dim(cells, cells.shape[dim] - width, cells.shape[dim], axis=dim)
        cells = jnp.concatenate(
            [
                lax.ppermute(tail, axis, [(i, (i + 1) % count) for i in range(ends)]),
                cells,
                lax.ppermute(head, axis, [((i + 1) % count, i) for i in range(ends)]),
            ],
            axis=dim,
        )
    return cells


def from_behind(value, axis, steps):
    count = lax.axis_size(axis)
    first, last = (max(0, -steps), min(count, count - steps))
    return lax.ppermute(value, axis, [(source, source + steps) for source in range(first, last)])


def project_all(normed, query_weight, key_weight, value_weight, lead, positions, chans):
    query = (
        jnp.dot(normed, query_weight, preferred_element_type=jnp.float32)
        .astype(jnp.bfloat16)
        .reshape(lead, positions, chans)
    )
    key = (
        jnp.dot(normed, key_weight, preferred_element_type=jnp.float32)
        .astype(jnp.bfloat16)
        .reshape(lead, positions, chans)
    )
    value = (
        jnp.dot(normed, value_weight, preferred_element_type=jnp.float32)
        .astype(jnp.bfloat16)
        .reshape(lead, positions, chans)
    )
    return (query, key, value)


def on_device(
    frames_in,
    spatial_kernel,
    temporal_kernel,
    norm_gain,
    query_weight,
    key_weight,
    value_weight,
    out_weight,
    cotangent,
):
    frames, rows, cols, chans = frames_in.shape
    padded = extended_2(frames_in, (("space", 1),), 1)
    padded = jnp.pad(padded, ((0, 0), (0, 0), (1, 1), (0, 0)))
    spatial = jnp.zeros((frames * rows * cols, chans), jnp.float32)
    for di in range(3):
        for dj in range(3):
            piece = padded[:, di : di + rows, dj : dj + cols, :].reshape(-1, chans)
            spatial = spatial + jnp.dot(
                piece, spatial_kernel[di, dj], preferred_element_type=jnp.float32
            )
    act = jax.nn.silu(spatial).astype(jnp.bfloat16).reshape(frames, rows, cols, chans)
    earlier = from_behind(act[frames - 2 :], "tm", 1)
    extended = jnp.concatenate([earlier, act], axis=0)
    temporal = jnp.zeros((frames * rows * cols, chans), jnp.float32)
    flat_grad = cotangent.reshape(-1, chans)
    grads = []
    for tap in range(3):
        shifted = extended[2 - tap : 2 - tap + frames].reshape(-1, chans)
        temporal = temporal + jnp.dot(
            shifted, temporal_kernel[tap], preferred_element_type=jnp.float32
        )
        grads.append(
            jnp.einsum("nc,nd->cd", shifted, flat_grad, preferred_element_type=jnp.float32)
        )
    partial_grad = jnp.stack(grads, axis=0)
    hidden = (frames_in.reshape(-1, chans).astype(jnp.float32) + temporal).astype(jnp.bfloat16)
    parts = lax.axis_size("tm")
    all_frames = frames * parts
    positions = rows * cols // parts
    moved = lax.all_to_all(
        hidden.reshape(frames, parts * positions, chans), "tm", 1, 0, tiled=True
    ).reshape(all_frames * positions, chans)
    wide = moved.astype(jnp.float32)
    normed = (
        wide / jnp.sqrt(jnp.mean(wide * wide, axis=1, keepdims=True) + 1e-06) * norm_gain
    ).astype(jnp.bfloat16)
    query, key, value = project_all(
        normed, query_weight, key_weight, value_weight, all_frames, positions, chans
    )
    scale = 1.0 / jnp.sqrt(jnp.float32(chans))
    scores = jnp.einsum("anc,bnc->nab", query, key, preferred_element_type=jnp.float32) * scale
    order = jnp.arange(all_frames)
    allowed = (order[None, :] <= order[:, None])[None, :, :]
    masked = jnp.where(allowed, scores, jnp.float32(-1e30))
    expon = jnp.where(
        allowed, jnp.exp(scores - jnp.max(masked, axis=2, keepdims=True)), jnp.float32(0.0)
    )
    share = (expon / jnp.sum(expon, axis=2, keepdims=True)).astype(jnp.bfloat16)
    attended = jnp.einsum("nab,bnc->anc", share, value, preferred_element_type=jnp.float32).astype(
        jnp.bfloat16
    )
    encoded = (
        wide + jnp.dot(attended.reshape(-1, chans), out_weight, preferred_element_type=jnp.float32)
    ).astype(jnp.bfloat16)
    encoded = lax.all_to_all(
        encoded.reshape(all_frames, positions, chans), "tm", 0, 1, tiled=True
    )
    over = lax.axis_size("space")
    blocks = partial_grad.reshape(3, parts, chans // parts, over, chans // over)
    blocks = blocks.transpose(3, 1, 0, 2, 4).reshape(-1, chans)
    section = lax.psum_scatter(blocks, "space", scatter_dimension=0, tiled=True)
    kernel_grad = lax.psum_scatter(section, "tm", scatter_dimension=0, tiled=True)
    kernel_grad = kernel_grad.reshape(3, chans // parts, chans // over)
    return (encoded.reshape(frames, rows, cols, chans), kernel_grad)


def solution(mesh):
    in_specs = (
        P("tm", "space", None, None),
        P(),
        P(),
        P(),
        P(),
        P(),
        P(),
        P(),
        P("tm", "space", None, None),
    )
    out_specs = (P("tm", "space", None, None), P(None, "tm", "space"))
    return jax.shard_map(
        on_device, mesh=mesh, in_specs=in_specs, out_specs=out_specs, check_vma=False
    )
```

```python
import functools

import jax
import jax.numpy as jnp
from jax import lax
from jax.experimental import pallas as pl
from jax.experimental.pallas import tpu as pltpu
from jax.sharding import PartitionSpec as P

F32 = jnp.float32
BF16 = jnp.bfloat16
MESH = pl.DeviceIdType.MESH
CH = 512
TAPS = 3 * CH


def remote(src, dst, send_sem, recv_sem, device):
    return pltpu.make_async_remote_copy(
        src_ref=src,
        dst_ref=dst,
        send_sem=send_sem,
        recv_sem=recv_sem,
        device_id=device,
        device_id_type=MESH,
    )


def kernel(
    x_ref,
    wsp_ref,
    wt_ref,
    gain_ref,
    wq_ref,
    wk_ref,
    wv_ref,
    wo_ref,
    cot_ref,
    enc_ref,
    kg_ref,
    xpad,
    w2,
    wt,
    wq,
    wk,
    wv,
    wo,
    cot,
    cot_t,
    ext,
    ybuf,
    hid,
    hall,
    nrm,
    qb,
    kb,
    vb,
    sbuf,
    pbuf,
    ab,
    enc,
    part,
    a1,
    r1,
    a2,
    r2,
    a3,
    b4,
    a4,
    fin,
    w_sem,
    l_sem,
    row_send,
    row_recv,
    time_send,
    time_recv,
    hid_send,
    hid_recv,
    hid_own,
    enc_send,
    enc_recv,
    enc_own,
    s1_send,
    s1_recv,
    s2_send,
    s2_recv,
    s3_send,
    s3_recv,
    s4_send,
    s4_recv,
):
    t = lax.axis_index("tm")
    s = lax.axis_index("space")
    core = s % 2
    z = (s // 2) % 4
    y = s // 8

    own_x = pltpu.make_async_copy(x_ref, xpad.at[:, 64:320], l_sem.at[0])
    own_x.start()
    w_loads = []
    for dj in range(3):
        for di in range(3):
            load = pltpu.make_async_copy(
                wsp_ref.at[di, dj], w2.at[dj, di * CH : (di + 1) * CH], w_sem.at[3 * dj + di]
            )
            load.start()
            w_loads.append(load)
    loads = []
    for i, (src, dst) in enumerate(
        ((cot_ref, cot), (wt_ref, wt), (wq_ref, wq), (wk_ref, wk), (wv_ref, wv), (wo_ref, wo))
    ):
        load = pltpu.make_async_copy(src, dst, l_sem.at[1 + i])
        load.start()
        loads.append(load)

    below = {"space": (s + 1) % 16}
    above = {"space": (s + 15) % 16}
    z_peers = [{"space": y * 8 + ((z + o) % 4) * 2 + core} for o in range(1, 4)]
    y_peer = {"space": (1 - y) * 8 + z * 2 + core}
    core_peer = {"space": s + 1 - 2 * core}
    t_peers = [{"tm": (t + o) % 8} for o in range(1, 8)]

    barrier = pltpu.get_barrier_semaphore()
    for peer in [below, above, y_peer] + z_peers + t_peers:
        pl.semaphore_signal(barrier, inc=1, device_id=peer, device_id_type=MESH)
    pl.semaphore_wait(barrier, 13)

    to_below = remote(
        x_ref.at[:, 192:256], xpad.at[:, 0:64], row_send.at[0], row_recv.at[0], below
    )
    to_above = remote(
        x_ref.at[:, 0:64], xpad.at[:, 320:384], row_send.at[1], row_recv.at[1], above
    )
    to_below.start()
    to_above.start()

    column = lax.broadcasted_iota(jnp.int32, (64, 256), 0)

    def activate(chunks, place):
        def body(i, carry):
            frame, row = place(i)
            start = pl.multiple_of(i * 64, 64)
            to = pl.multiple_of(row * 64, 64)
            for half in range(2):
                lanes = slice(half * 256, half * 256 + 256)
                left = pltpu.roll(ybuf[0, pl.ds(start, 64), lanes], 1, 0)
                mid = ybuf[1, pl.ds(start, 64), lanes]
                right = pltpu.roll(ybuf[2, pl.ds(start, 64), lanes], 63, 0)
                v = mid + jnp.where(column == 0, 0.0, left) + jnp.where(column == 63, 0.0, right)
                ext[frame + 2, pl.ds(to, 64), lanes] = (v / (1.0 + jnp.exp(-v))).astype(BF16)
            return carry

        lax.fori_loop(0, chunks, body, 0)

    own_x.wait()
    for dj in range(3):
        for di in range(3):
            w_loads[3 * dj + di].wait()
        lhs = jnp.concatenate(
            [
                xpad[:, 64 * (1 + di) : 64 * (1 + di) + 128, :].reshape(512, CH)
                for di in range(3)
            ],
            axis=1,
        )
        ybuf[dj] = jnp.dot(lhs, w2[dj], preferred_element_type=F32)
    activate(8, lambda i: (i // 2, 1 + i % 2))

    loads[0].wait()
    for i in range(4):
        cot_t[:, 256 * i : 256 * i + 256] = cot[256 * i : 256 * i + 256, :].T

    to_below.wait()
    to_above.wait()

    @pl.when(s == 0)
    def _():
        xpad[:, 0:64, :] = jnp.zeros((4, 64, CH), BF16)

    @pl.when(s == 15)
    def _():
        xpad[:, 320:384, :] = jnp.zeros((4, 64, CH), BF16)

    def edges(first):
        for dj in range(3):
            lhs = jnp.concatenate(
                [
                    jnp.concatenate(
                        [
                            xpad[first : first + 2, 64 * di : 64 * di + 64, :],
                            xpad[first : first + 2, 64 * (3 + di) : 64 * (3 + di) + 64, :],
                        ],
                        axis=1,
                    ).reshape(256, CH)
                    for di in range(3)
                ],
                axis=1,
            )
            ybuf[dj, 0:256] = jnp.dot(lhs, w2[dj], preferred_element_type=F32)
        activate(4, lambda i: (first + i // 2, 3 * (i % 2)))

    edges(2)
    later = remote(
        ext.at[4:6], ext.at[0:2], time_send.at[0], time_recv.at[0], {"tm": (t + 1) % 8}
    )
    later.start()
    edges(0)

    loads[1].wait()

    def hidden(first):
        lhs = jnp.concatenate(
            [ext[first + 2 - k : first + 4 - k].reshape(512, CH) for k in range(3)], axis=1
        )
        temporal = jnp.dot(lhs, wt[...], preferred_element_type=F32)
        value = xpad[first : first + 2, 64:320, :].reshape(512, CH).astype(F32) + temporal
        value = value.astype(BF16)
        for f in range(2):
            hid[:, :, first + f] = value[256 * f : 256 * f + 256].reshape(8, 2, 16, CH)

    def hid_copies(first, g):
        pair = first // 2
        here = pl.ds(t * 4 + first, 2)
        copies = []
        for o in range(1, 8):
            copies.append(
                remote(
                    hid.at[(t + o) % 8, g, first : first + 2],
                    hall.at[g, here],
                    hid_send.at[pair, g, o - 1],
                    hid_recv.at[pair, g, o - 1],
                    t_peers[o - 1],
                )
            )
        own = pltpu.make_async_copy(
            hid.at[t, g, first : first + 2], hall.at[g, here], hid_own.at[pair, g]
        )
        return copies, own

    def send_hidden(first):
        started = []
        for g in range(2):
            copies, own = hid_copies(first, g)
            for copy in copies:
                copy.start()
            own.start()
            started.append((copies, own))
        return started

    hidden(2)
    hid_late = send_hidden(2)

    def tap(k):
        shifted = ext[2 - k : 6 - k].reshape(1024, CH)
        grad = jnp.dot(cot_t[...], shifted, preferred_element_type=F32).astype(BF16)
        part[:, :, :, k * CH : (k + 1) * CH] = grad.reshape(8, 2, 32, CH)

    tap(0)
    stage1 = [
        remote(
            part.at[:, 1 - core, :, lanes],
            a1.at[:, :, lanes],
            s1_send.at[i],
            s1_recv.at[i],
            core_peer,
        )
        for i, lanes in enumerate((slice(0, CH), slice(CH, TAPS)))
    ]
    stage1[0].start()

    later.wait()

    @pl.when(t == 0)
    def _():
        ext[0:2] = jnp.zeros((2, 256, CH), BF16)

    hidden(0)
    hid_early = send_hidden(0)

    tap(1)
    tap(2)
    stage1[1].start()
    for copy in stage1:
        copy.wait()
    for i in range(8):
        r1[i // 4, i % 4] = (part[i, core].astype(F32) + a1[i].astype(F32)).astype(BF16)
    stage2 = [
        remote(
            r1.at[:, (z + o) % 4], a2.at[o - 1], s2_send.at[o - 1], s2_recv.at[o - 1], z_peers[o - 1]
        )
        for o in range(1, 4)
    ]
    for copy in stage2:
        copy.start()

    for load in loads[2:]:
        load.wait()

    scale = 1.0 / (CH**0.5)

    def project(g):
        for started in (hid_late, hid_early):
            copies, own = started[g]
            for copy in copies:
                copy.wait_recv()
            own.wait()
        def norm_rows(i, carry):
            wide = hall[g, pl.ds(i * 8, 8)].reshape(128, CH).astype(F32)
            inv = 1.0 / jnp.sqrt(jnp.mean(wide * wide, axis=1, keepdims=True) + 1e-06)
            rows = pl.ds(pl.multiple_of(i * 128, 128), 128)
            nrm[rows, :] = (wide * inv * gain_ref[...]).astype(BF16)
            return carry

        lax.fori_loop(0, 4, norm_rows, 0)
        for weight, out in ((wq, qb), (wk, kb), (wv, vb)):
            out[...] = jnp.dot(nrm[...], weight[...], preferred_element_type=F32).astype(BF16)

    def attend(g, tile):
        keys = 256 * (tile + 1)
        base = 256 * tile
        sbuf[:, :keys] = lax.dot_general(
            qb[base : base + 256, :],
            kb[:keys, :],
            (((1,), (1,)), ((), ())),
            preferred_element_type=F32,
        )

        def soft(i, carry):
            rows = pl.ds(pl.multiple_of(i * 64, 64), 64)
            scores = sbuf[rows, :keys] * scale
            row = lax.broadcasted_iota(jnp.int32, (64, keys), 0) + (base + i * 64)
            col = lax.broadcasted_iota(jnp.int32, (64, keys), 1)
            allowed = (((row ^ col) & 15) == 0) & (col <= row)
            scores = jnp.where(allowed, scores, -1e30)
            expon = jnp.where(
                allowed, jnp.exp(scores - jnp.max(scores, axis=1, keepdims=True)), 0.0
            )
            total = jnp.sum(expon, axis=1, keepdims=True)
            pbuf[rows, :keys] = (expon * (1.0 / total)).astype(BF16)
            return carry

        lax.fori_loop(0, 4, soft, 0)
        ab[...] = jnp.dot(pbuf[:, :keys], vb[:keys, :], preferred_element_type=F32).astype(BF16)
        back = jnp.dot(ab[...], wo[...], preferred_element_type=F32)
        frames = slice(16 * tile, 16 * tile + 16)
        wide = hall[g, frames].reshape(256, CH).astype(F32)
        enc[g, frames] = (wide + back).astype(BF16).reshape(16, 16, CH)

    def enc_copy(g, o):
        p = (t + o) % 8
        return remote(
            enc.at[g, pl.ds(p * 4, 4)],
            enc_ref.at[:, t, g],
            enc_send.at[g, o],
            enc_recv.at[g, o],
            {"tm": p},
        )

    def enc_local(g):
        return pltpu.make_async_copy(
            enc.at[g, pl.ds(t * 4, 4)], enc_ref.at[:, t, g], enc_own.at[g]
        )

    def send_encoded(g, tile):
        for o in range(8):
            p = (t + o) % 8

            @pl.when(p // 4 == tile)
            def _():
                if o == 0:
                    enc_local(g).start()
                else:
                    enc_copy(g, o).start()

    project(0)
    attend(0, 0)
    send_encoded(0, 0)
    for copy in stage2:
        copy.wait()
    for i in range(2):
        r2[i] = (
            r1[i, z].astype(F32)
            + a2[0, i].astype(F32)
            + a2[1, i].astype(F32)
            + a2[2, i].astype(F32)
        ).astype(BF16)
    stage3 = remote(r2.at[1 - y], a3, s3_send.at[0], s3_recv.at[0], y_peer)
    stage3.start()
    attend(0, 1)
    send_encoded(0, 1)

    project(1)
    stage3.wait()
    for k in range(3):
        for q in range(4):
            lanes = slice(k * CH + q * 128, k * CH + q * 128 + 128)
            b4[q, k] = (r2[y, :, lanes].astype(F32) + a3[:, lanes].astype(F32)).astype(BF16)
    stage4 = [
        remote(
            b4.at[((t + o) % 8) // 2],
            a4.at[o - 1],
            s4_send.at[o - 1],
            s4_recv.at[o - 1],
            t_peers[o - 1],
        )
        for o in range(1, 8)
    ]
    for copy in stage4:
        copy.start()
    attend(1, 0)
    send_encoded(1, 0)
    attend(1, 1)
    send_encoded(1, 1)

    for copy in stage4:
        copy.wait()
    for k in range(3):
        total = b4[t // 2, k].astype(F32)
        for o in range(7):
            total = total + a4[o, k].astype(F32)
        fin[k] = total.T
    kg_ref[...] = fin[:, pl.ds(pl.multiple_of((t % 2) * 64, 64), 64), :]

    for started in hid_late + hid_early:
        for copy in started[0]:
            copy.wait_send()
    for g in range(2):
        enc_local(g).wait()
        for o in range(1, 8):
            enc_copy(g, o).wait()


def on_device(
    frames_in,
    spatial_kernel,
    temporal_kernel,
    norm_gain,
    query_weight,
    key_weight,
    value_weight,
    out_weight,
    cotangent,
):
    frames, rows, cols, chans = frames_in.shape
    anywhere = pl.BlockSpec(memory_space=pl.ANY)
    vmem = pl.BlockSpec(memory_space=pltpu.VMEM)
    dma = pltpu.SemaphoreType.DMA
    square = pltpu.VMEM((CH, CH), BF16)
    encoded, grad = pl.pallas_call(
        kernel,
        name="block",
        out_shape=(
            jax.ShapeDtypeStruct((4, 8, 2, 16, CH), BF16),
            jax.ShapeDtypeStruct((3, 64, 32), F32),
        ),
        in_specs=[anywhere] * 3 + [vmem] + [anywhere] * 5,
        out_specs=(anywhere, vmem),
        scratch_shapes=[
            pltpu.VMEM((4, 384, CH), BF16),
            pltpu.VMEM((3, TAPS, CH), BF16),
            pltpu.VMEM((TAPS, CH), BF16),
            square,
            square,
            square,
            square,
            pltpu.VMEM((1024, CH), BF16),
            pltpu.VMEM((CH, 1024), BF16),
            pltpu.VMEM((6, 256, CH), BF16),
            pltpu.VMEM((3, 512, CH), F32),
            pltpu.VMEM((8, 2, 4, 16, CH), BF16),
            pltpu.VMEM((2, 32, 16, CH), BF16),
            square,
            square,
            square,
            square,
            pltpu.VMEM((256, 512), F32),
            pltpu.VMEM((256, 512), BF16),
            pltpu.VMEM((256, CH), BF16),
            pltpu.VMEM((2, 32, 16, CH), BF16),
            pltpu.VMEM((8, 2, 32, TAPS), BF16),
            pltpu.VMEM((8, 32, TAPS), BF16),
            pltpu.VMEM((2, 4, 32, TAPS), BF16),
            pltpu.VMEM((3, 2, 32, TAPS), BF16),
            pltpu.VMEM((2, 32, TAPS), BF16),
            pltpu.VMEM((32, TAPS), BF16),
            pltpu.VMEM((4, 3, 32, 128), BF16),
            pltpu.VMEM((7, 3, 32, 128), BF16),
            pltpu.VMEM((3, 128, 32), F32),
            dma((9,)),
            dma((7,)),
            dma((2,)),
            dma((2,)),
            dma((1,)),
            dma((1,)),
            dma((2, 2, 7)),
            dma((2, 2, 7)),
            dma((2, 2)),
            dma((2, 8)),
            dma((2, 8)),
            dma((2,)),
            dma((2,)),
            dma((2,)),
            dma((3,)),
            dma((3,)),
            dma((1,)),
            dma((1,)),
            dma((7,)),
            dma((7,)),
        ],
        compiler_params=pltpu.CompilerParams(
            collective_id=0, has_side_effects=True, vmem_limit_bytes=60 * 1024 * 1024
        ),
    )(
        frames_in.reshape(frames, rows * cols, chans),
        spatial_kernel,
        temporal_kernel.reshape(3 * chans, chans),
        norm_gain.reshape(1, chans),
        query_weight,
        key_weight,
        value_weight,
        out_weight,
        cotangent.reshape(-1, chans),
    )
    return (encoded.reshape(frames, rows, cols, chans), grad)


def solution(mesh):
    tile = P("tm", "space", None, None)
    in_specs = (tile, P(), P(), P(), P(), P(), P(), P(), tile)
    out_specs = (tile, P(None, "tm", "space"))
    return jax.shard_map(
        on_device, mesh=mesh, in_specs=in_specs, out_specs=out_specs, check_vma=False
    )
```

```python
import functools

import jax
import jax.numpy as jnp
from jax import lax
from jax.experimental import pallas as pl
from jax.experimental.pallas import tpu as pltpu
from jax.sharding import PartitionSpec as P

F32 = jnp.float32
BF16 = jnp.bfloat16
MESH = pl.DeviceIdType.MESH
CH = 512
TAPS = 3 * CH


def remote(src, dst, send_sem, recv_sem, device):
    return pltpu.make_async_remote_copy(
        src_ref=src,
        dst_ref=dst,
        send_sem=send_sem,
        recv_sem=recv_sem,
        device_id=device,
        device_id_type=MESH,
    )


def kernel(
    x_ref,
    wsp_ref,
    wt_ref,
    gain_ref,
    wq_ref,
    wk_ref,
    wv_ref,
    wo_ref,
    cot_ref,
    enc_ref,
    kg_ref,
    xpad,
    w2,
    wt,
    wq,
    wk,
    wv,
    wo,
    cot,
    cot_t,
    ext,
    ybuf,
    hid,
    hall,
    nrm,
    qb,
    kb,
    vb,
    sbuf,
    pbuf,
    ab,
    enc,
    part,
    a1,
    r1,
    a2,
    r2,
    a3,
    b4,
    a4,
    w_sem,
    l_sem,
    row_send,
    row_recv,
    time_send,
    time_recv,
    hid_send,
    hid_recv,
    hid_own,
    enc_send,
    enc_recv,
    enc_own,
    s1_send,
    s1_recv,
    s2_send,
    s2_recv,
    s3_send,
    s3_recv,
    s4_send,
    s4_recv,
):
    t = lax.axis_index("tm")
    s = lax.axis_index("space")
    core = s % 2
    z = (s // 2) % 4
    y = s // 8

    below = {"space": (s + 1) % 16}
    above = {"space": (s + 15) % 16}
    z_peers = [{"space": y * 8 + ((z + o) % 4) * 2 + core} for o in range(1, 4)]
    y_peer = {"space": (1 - y) * 8 + z * 2 + core}
    core_peer = {"space": s + 1 - 2 * core}
    t_peers = [{"tm": (t + o) % 8} for o in range(1, 8)]

    barrier = pltpu.get_barrier_semaphore()
    for peer in [below, above, y_peer] + z_peers + t_peers:
        pl.semaphore_signal(barrier, inc=1, device_id=peer, device_id_type=MESH)

    own_x = pltpu.make_async_copy(x_ref, xpad.at[:, 64:320], l_sem.at[0])
    own_x.start()
    w_loads = []
    for dj in range(3):
        for di in range(3):
            load = pltpu.make_async_copy(
                wsp_ref.at[di, dj], w2.at[dj, di * CH : (di + 1) * CH], w_sem.at[3 * dj + di]
            )
            load.start()
            w_loads.append(load)
    loads = []
    for i, (src, dst) in enumerate(
        ((cot_ref, cot), (wt_ref, wt), (wq_ref, wq), (wk_ref, wk), (wv_ref, wv), (wo_ref, wo))
    ):
        loads.append(pltpu.make_async_copy(src, dst, l_sem.at[1 + i]))

    rows_in = {}
    for first in (2, 0):
        frames = slice(first, first + 2)
        pair = first // 2
        rows_in[first] = [
            remote(
                x_ref.at[frames, 192:256],
                xpad.at[frames, 0:64],
                row_send.at[pair, 0],
                row_recv.at[pair, 0],
                below,
            ),
            remote(
                x_ref.at[frames, 0:64],
                xpad.at[frames, 320:384],
                row_send.at[pair, 1],
                row_recv.at[pair, 1],
                above,
            ),
        ]

    column = lax.broadcasted_iota(jnp.int32, (64, 256), 0)

    def activate(place):
        def body(i, carry):
            frame, row = place(i)
            start = pl.multiple_of(i * 64, 64)
            to = pl.multiple_of(row * 64, 64)
            for half in range(2):
                lanes = slice(half * 256, half * 256 + 256)
                left = pltpu.roll(ybuf[0, pl.ds(start, 64), lanes], 1, 0)
                mid = ybuf[1, pl.ds(start, 64), lanes]
                right = pltpu.roll(ybuf[2, pl.ds(start, 64), lanes], 63, 0)
                v = mid + jnp.where(column == 0, 0.0, left) + jnp.where(column == 63, 0.0, right)
                ext[frame + 2, pl.ds(to, 64), lanes] = (v / (1.0 + jnp.exp(-v))).astype(BF16)
            return carry

        lax.fori_loop(0, 4, body, 0)

    def middle(first, weights=()):
        for dj in range(3):
            for load in weights[3 * dj : 3 * dj + 3]:
                load.wait()
            lhs = jnp.concatenate(
                [
                    xpad[first : first + 2, 64 * (1 + di) : 64 * (1 + di) + 128, :].reshape(256, CH)
                    for di in range(3)
                ],
                axis=1,
            )
            ybuf[dj] = jnp.dot(lhs, w2[dj], preferred_element_type=F32)
        activate(lambda i: (first + i // 2, 1 + i % 2))

    def edges(first):
        @pl.when(s > 0)
        def _():
            rows_in[first][0].wait_recv()

        @pl.when(s < 15)
        def _():
            rows_in[first][1].wait_recv()

        @pl.when(s == 0)
        def _():
            xpad[first : first + 2, 0:64, :] = jnp.zeros((2, 64, CH), BF16)

        @pl.when(s == 15)
        def _():
            xpad[first : first + 2, 320:384, :] = jnp.zeros((2, 64, CH), BF16)

        for dj in range(3):
            lhs = jnp.concatenate(
                [
                    jnp.concatenate(
                        [
                            xpad[first : first + 2, 64 * di : 64 * di + 64, :],
                            xpad[first : first + 2, 64 * (3 + di) : 64 * (3 + di) + 64, :],
                        ],
                        axis=1,
                    ).reshape(256, CH)
                    for di in range(3)
                ],
                axis=1,
            )
            ybuf[dj] = jnp.dot(lhs, w2[dj], preferred_element_type=F32)
        activate(lambda i: (first + i // 2, 3 * (i % 2)))

    later = [
        remote(
            ext.at[4:6, rows],
            ext.at[0:2, rows],
            time_send.at[i],
            time_recv.at[i],
            {"tm": (t + 1) % 8},
        )
        for i, rows in enumerate((slice(64, 192), slice(0, 64), slice(192, 256)))
    ]

    pl.semaphore_wait(barrier, 13)
    @pl.when(s < 15)
    def _():
        rows_in[2][0].start()
        rows_in[0][0].start()

    @pl.when(s > 0)
    def _():
        rows_in[2][1].start()
        rows_in[0][1].start()

    own_x.wait()
    def send_later(pieces):
        @pl.when(t < 7)
        def _():
            for copy in pieces:
                copy.start()

    middle(2, w_loads)
    send_later(later[:1])
    for load in loads:
        load.start()
    edges(2)
    send_later(later[1:])
    middle(0)
    edges(0)

    loads[1].wait()

    def hidden(first):
        lhs = jnp.concatenate(
            [ext[first + 2 - k : first + 4 - k].reshape(512, CH) for k in range(3)], axis=1
        )
        temporal = jnp.dot(lhs, wt[...], preferred_element_type=F32)
        value = xpad[first : first + 2, 64:320, :].reshape(512, CH).astype(F32) + temporal
        value = value.astype(BF16)
        for f in range(2):
            hid[:, :, first + f] = value[256 * f : 256 * f + 256].reshape(8, 2, 16, CH)

    def hid_copies(first, g):
        pair = first // 2
        copies = []
        for o in range(1, 8):
            copies.append(
                remote(
                    hid.at[(t + o) % 8, g, first : first + 2],
                    hall.at[g, t, first : first + 2],
                    hid_send.at[pair, g, o - 1],
                    hid_recv.at[pair, g, o - 1],
                    t_peers[o - 1],
                )
            )
        own = pltpu.make_async_copy(
            hid.at[t, g, first : first + 2], hall.at[g, t, first : first + 2], hid_own.at[pair, g]
        )
        return copies, own

    hid_late = [hid_copies(2, g) for g in range(2)]
    hid_early = [hid_copies(0, g) for g in range(2)]

    def send_hidden(exchange):
        copies, own = exchange
        for copy in copies:
            copy.start()
        own.start()

    hidden(2)
    send_hidden(hid_late[0])

    loads[0].wait()
    for i in range(4):
        cot_t[:, 256 * i : 256 * i + 256] = cot[256 * i : 256 * i + 256, :].T

    def tap(k):
        shifted = ext[2 - k : 6 - k].reshape(1024, CH)
        grad = jnp.dot(cot_t[...], shifted, preferred_element_type=F32).astype(BF16)
        part[:, :, :, k * CH : (k + 1) * CH] = grad.reshape(8, 2, 32, CH)

    tap(0)
    stage1 = [
        remote(
            part.at[:, 1 - core, :, lanes],
            a1.at[:, :, lanes],
            s1_send.at[i],
            s1_recv.at[i],
            core_peer,
        )
        for i, lanes in enumerate((slice(0, CH), slice(CH, TAPS)))
    ]
    stage1[0].start()

    @pl.when(t > 0)
    def _():
        for copy in later:
            copy.wait_recv()

    @pl.when(t == 0)
    def _():
        ext[0:2] = jnp.zeros((2, 256, CH), BF16)

    hidden(0)
    send_hidden(hid_early[0])
    send_hidden(hid_late[1])
    send_hidden(hid_early[1])

    tap(1)
    tap(2)
    stage1[1].start()
    scale = 1.0 / (CH**0.5)

    for load in loads[2:]:
        load.wait()

    def project(started, first, g):
        copies, own = started[g]
        for copy in copies:
            copy.wait_recv()
        own.wait()

        def norm_rows(i, carry):
            wide = hall[g, pl.ds(i * 4, 4), first : first + 2].reshape(128, CH).astype(F32)
            inv = 1.0 / jnp.sqrt(jnp.mean(wide * wide, axis=1, keepdims=True) + 1e-06)
            rows = pl.ds(pl.multiple_of(i * 128, 128), 128)
            nrm[rows, :] = (wide * inv * gain_ref[...]).astype(BF16)
            return carry

        lax.fori_loop(0, 2, norm_rows, 0)
        for weight, out in ((wq, qb), (wk, kb), (wv, vb)):
            value = jnp.dot(nrm[...], weight[...], preferred_element_type=F32).astype(BF16)
            out[g, :, first : first + 2] = value.reshape(8, 2, 16, CH)

    def attend(g, tile):
        keys = 256 * (tile + 1)
        base = 256 * tile
        sbuf[:, :keys] = lax.dot_general(
            qb[g, 4 * tile : 4 * tile + 4].reshape(256, CH),
            kb[g, : 4 * tile + 4].reshape(keys, CH),
            (((1,), (1,)), ((), ())),
            preferred_element_type=F32,
        )

        def soft(i, carry):
            rows = pl.ds(pl.multiple_of(i * 64, 64), 64)
            scores = sbuf[rows, :keys] * scale
            row = lax.broadcasted_iota(jnp.int32, (64, keys), 0) + (base + i * 64)
            col = lax.broadcasted_iota(jnp.int32, (64, keys), 1)
            allowed = (((row ^ col) & 15) == 0) & (col <= row)
            scores = jnp.where(allowed, scores, -1e30)
            expon = jnp.where(
                allowed, jnp.exp(scores - jnp.max(scores, axis=1, keepdims=True)), 0.0
            )
            total = jnp.sum(expon, axis=1, keepdims=True)
            pbuf[rows, :keys] = (expon * (1.0 / total)).astype(BF16)
            return carry

        lax.fori_loop(0, 4, soft, 0)
        values = vb[g, : 4 * tile + 4].reshape(keys, CH)
        ab[...] = jnp.dot(pbuf[:, :keys], values, preferred_element_type=F32).astype(BF16)
        back = jnp.dot(ab[...], wo[...], preferred_element_type=F32)
        frames = slice(16 * tile, 16 * tile + 16)
        wide = hall[g, 4 * tile : 4 * tile + 4].reshape(256, CH).astype(F32)
        enc[g, frames] = (wide + back).astype(BF16).reshape(16, 16, CH)

    def enc_copy(g, o):
        p = (t + o) % 8
        return remote(
            enc.at[g, pl.ds(p * 4, 4)],
            enc_ref.at[:, t, g],
            enc_send.at[g, o],
            enc_recv.at[g, o],
            {"tm": p},
        )

    def enc_local(g):
        return pltpu.make_async_copy(
            enc.at[g, pl.ds(t * 4, 4)], enc_ref.at[:, t, g], enc_own.at[g]
        )

    def send_encoded(g, tile):
        for o in range(8):
            p = (t + o) % 8

            @pl.when(p // 4 == tile)
            def _():
                if o == 0:
                    enc_local(g).start()
                else:
                    enc_copy(g, o).start()

    project(hid_late, 2, 0)
    for copy in stage1:
        copy.wait()
    for i in range(8):
        r1[i // 4, i % 4] = (part[i, core].astype(F32) + a1[i].astype(F32)).astype(BF16)
    stage2 = [
        remote(
            r1.at[:, (z + o) % 4], a2.at[o - 1], s2_send.at[o - 1], s2_recv.at[o - 1], z_peers[o - 1]
        )
        for o in range(1, 4)
    ]
    for copy in stage2:
        copy.start()

    project(hid_early, 0, 0)
    attend(0, 0)
    send_encoded(0, 0)
    attend(0, 1)
    send_encoded(0, 1)
    project(hid_late, 2, 1)
    project(hid_early, 0, 1)
    attend(1, 0)
    send_encoded(1, 0)
    attend(1, 1)
    send_encoded(1, 1)
    for copy in stage2:
        copy.wait()
    for i in range(2):
        r2[i] = (
            r1[i, z].astype(F32)
            + a2[0, i].astype(F32)
            + a2[1, i].astype(F32)
            + a2[2, i].astype(F32)
        ).astype(BF16)
    stage3 = remote(r2.at[1 - y], a3, s3_send.at[0], s3_recv.at[0], y_peer)
    stage3.start()
    stage3.wait()
    for k in range(3):
        for q in range(4):
            lanes = slice(k * CH + q * 128, k * CH + q * 128 + 128)
            b4[q, k] = (r2[y, :, lanes].astype(F32) + a3[:, lanes].astype(F32)).astype(BF16)
    stage4 = [
        remote(
            b4.at[((t + o) % 8) // 2],
            a4.at[o - 1],
            s4_send.at[o - 1],
            s4_recv.at[o - 1],
            t_peers[o - 1],
        )
        for o in range(1, 8)
    ]
    for copy in stage4:
        copy.start()

    for copy in stage4:
        copy.wait()
    for k in range(3):
        total = b4[t // 2, k].astype(F32)
        for o in range(7):
            total = total + a4[o, k].astype(F32)
        kg_ref[k] = jnp.where(t % 2 == 0, total[:, :64], total[:, 64:])

    @pl.when(s < 15)
    def _():
        rows_in[2][0].wait_send()
        rows_in[0][0].wait_send()

    @pl.when(s > 0)
    def _():
        rows_in[2][1].wait_send()
        rows_in[0][1].wait_send()

    @pl.when(t < 7)
    def _():
        for copy in later:
            copy.wait_send()

    for started in hid_late + hid_early:
        for copy in started[0]:
            copy.wait_send()
    for g in range(2):
        enc_local(g).wait()
        for o in range(1, 8):
            enc_copy(g, o).wait()


def place(enc_ref, kg_ref, enc_out, kg_out, held, held_grad, in_sem, out_sem):
    pieces = [(enc_ref.at[f], held.at[f], enc_out.at[f]) for f in range(4)]
    pieces.append((kg_ref, held_grad, kg_out))
    loads = [pltpu.make_async_copy(a, b, in_sem.at[i]) for i, (a, b, _) in enumerate(pieces)]
    stores = [pltpu.make_async_copy(b, c, out_sem.at[i]) for i, (_, b, c) in enumerate(pieces)]
    for load in loads:
        load.start()
    for load, store in zip(loads, stores):
        load.wait()
        store.start()
    for store in stores:
        store.wait()


def on_device(
    frames_in,
    spatial_kernel,
    temporal_kernel,
    norm_gain,
    query_weight,
    key_weight,
    value_weight,
    out_weight,
    cotangent,
):
    frames, rows, cols, chans = frames_in.shape
    anywhere = pl.BlockSpec(memory_space=pl.ANY)
    vmem = pl.BlockSpec(memory_space=pltpu.VMEM)
    dma = pltpu.SemaphoreType.DMA
    square = pltpu.VMEM((CH, CH), BF16)
    encoded, grad = pl.pallas_call(
        kernel,
        name="block",
        out_shape=(
            jax.ShapeDtypeStruct((4, 8, 2, 16, CH), BF16),
            jax.ShapeDtypeStruct((3, 32, 64), F32),
        ),
        in_specs=[anywhere] * 3 + [vmem] + [anywhere] * 5,
        out_specs=(anywhere, vmem),
        scratch_shapes=[
            pltpu.VMEM((4, 384, CH), BF16),
            pltpu.VMEM((3, TAPS, CH), BF16),
            pltpu.VMEM((TAPS, CH), BF16),
            square,
            square,
            square,
            square,
            pltpu.VMEM((1024, CH), BF16),
            pltpu.VMEM((CH, 1024), BF16),
            pltpu.VMEM((6, 256, CH), BF16),
            pltpu.VMEM((3, 256, CH), F32),
            pltpu.VMEM((8, 2, 4, 16, CH), BF16),
            pltpu.VMEM((2, 8, 4, 16, CH), BF16),
            pltpu.VMEM((256, CH), BF16),
            pltpu.VMEM((2, 8, 4, 16, CH), BF16),
            pltpu.VMEM((2, 8, 4, 16, CH), BF16),
            pltpu.VMEM((2, 8, 4, 16, CH), BF16),
            pltpu.VMEM((256, 512), F32),
            pltpu.VMEM((256, 512), BF16),
            pltpu.VMEM((256, CH), BF16),
            pltpu.VMEM((2, 32, 16, CH), BF16),
            pltpu.VMEM((8, 2, 32, TAPS), BF16),
            pltpu.VMEM((8, 32, TAPS), BF16),
            pltpu.VMEM((2, 4, 32, TAPS), BF16),
            pltpu.VMEM((3, 2, 32, TAPS), BF16),
            pltpu.VMEM((2, 32, TAPS), BF16),
            pltpu.VMEM((32, TAPS), BF16),
            pltpu.VMEM((4, 3, 32, 128), BF16),
            pltpu.VMEM((7, 3, 32, 128), BF16),
            dma((9,)),
            dma((7,)),
            dma((2, 2)),
            dma((2, 2)),
            dma((3,)),
            dma((3,)),
            dma((2, 2, 7)),
            dma((2, 2, 7)),
            dma((2, 2)),
            dma((2, 8)),
            dma((2, 8)),
            dma((2,)),
            dma((2,)),
            dma((2,)),
            dma((3,)),
            dma((3,)),
            dma((1,)),
            dma((1,)),
            dma((7,)),
            dma((7,)),
        ],
        compiler_params=pltpu.CompilerParams(
            collective_id=0, has_side_effects=True, vmem_limit_bytes=60 * 1024 * 1024
        ),
    )(
        frames_in.reshape(frames, rows * cols, chans),
        spatial_kernel,
        temporal_kernel.reshape(3 * chans, chans),
        norm_gain.reshape(1, chans),
        query_weight,
        key_weight,
        value_weight,
        out_weight,
        cotangent.reshape(-1, chans),
    )
    encoded, grad = pl.pallas_call(
        place,
        name="place",
        out_shape=(
            jax.ShapeDtypeStruct((frames, rows * cols, chans), BF16),
            jax.ShapeDtypeStruct((3, 32, 64), F32),
        ),
        in_specs=[anywhere] * 2,
        out_specs=(anywhere, anywhere),
        scratch_shapes=[
            pltpu.VMEM((4, 256, CH), BF16),
            pltpu.VMEM((3, 32, 64), F32),
            dma((5,)),
            dma((5,)),
        ],
        compiler_params=pltpu.CompilerParams(vmem_limit_bytes=60 * 1024 * 1024),
    )(encoded.reshape(frames, rows * cols, chans), grad)
    return (encoded.reshape(frames, rows, cols, chans), grad.transpose(0, 2, 1))


def solution(mesh):
    tile = P("tm", "space", None, None)
    in_specs = (tile, P(), P(), P(), P(), P(), P(), P(), tile)
    out_specs = (tile, P(None, "tm", "space"))
    return jax.shard_map(
        on_device, mesh=mesh, in_specs=in_specs, out_specs=out_specs, check_vma=False
    )
```

```python
import functools

import jax
import jax.numpy as jnp
from jax import lax
from jax.experimental import pallas as pl
from jax.experimental.pallas import tpu as pltpu
from jax.sharding import PartitionSpec as P

F32 = jnp.float32
BF16 = jnp.bfloat16
MESH = pl.DeviceIdType.MESH
CH = 512
TAPS = 3 * CH


def remote(src, dst, send_sem, recv_sem, device):
    return pltpu.make_async_remote_copy(
        src_ref=src,
        dst_ref=dst,
        send_sem=send_sem,
        recv_sem=recv_sem,
        device_id=device,
        device_id_type=MESH,
    )


def kernel(
    x_ref,
    wsp_ref,
    wt_ref,
    gain_ref,
    wq_ref,
    wk_ref,
    wv_ref,
    wo_ref,
    cot_ref,
    enc_ref,
    kg_ref,
    xpad,
    w2,
    wt,
    wq,
    wk,
    wv,
    wo,
    cot,
    cot_t,
    ext,
    ybuf,
    hid,
    hall,
    nrm,
    qb,
    kb,
    vb,
    sbuf,
    pbuf,
    ab,
    enc,
    part,
    a1,
    r1,
    a2,
    r2,
    a3,
    b4,
    a4,
    w_sem,
    l_sem,
    row_send,
    row_recv,
    time_send,
    time_recv,
    hid_send,
    hid_recv,
    hid_own,
    enc_send,
    enc_recv,
    enc_own,
    s1_send,
    s1_recv,
    s2_send,
    s2_recv,
    s3_send,
    s3_recv,
    s4_send,
    s4_recv,
):
    t = lax.axis_index("tm")
    s = lax.axis_index("space")
    core = s % 2
    z = (s // 2) % 4
    y = s // 8

    below = {"space": (s + 1) % 16}
    above = {"space": (s + 15) % 16}
    z_peers = [{"space": y * 8 + ((z + o) % 4) * 2 + core} for o in range(1, 4)]
    y_peer = {"space": (1 - y) * 8 + z * 2 + core}
    core_peer = {"space": s + 1 - 2 * core}
    t_peers = [{"tm": (t + o) % 8} for o in range(1, 8)]

    barrier = pltpu.get_barrier_semaphore()
    for peer in [below, above, y_peer] + z_peers + t_peers:
        pl.semaphore_signal(barrier, inc=1, device_id=peer, device_id_type=MESH)

    own_x = pltpu.make_async_copy(x_ref, xpad.at[:, 64:320], l_sem.at[0])
    own_x.start()
    w_loads = []
    for dj in range(3):
        for di in range(3):
            load = pltpu.make_async_copy(
                wsp_ref.at[di, dj], w2.at[dj, di * CH : (di + 1) * CH], w_sem.at[3 * dj + di]
            )
            load.start()
            w_loads.append(load)
    loads = []
    for i, (src, dst) in enumerate(
        ((cot_ref, cot), (wt_ref, wt), (wq_ref, wq), (wk_ref, wk), (wv_ref, wv), (wo_ref, wo))
    ):
        loads.append(pltpu.make_async_copy(src, dst, l_sem.at[1 + i]))

    rows_in = {}
    for first in (2, 0):
        frames = slice(first, first + 2)
        pair = first // 2
        rows_in[first] = [
            remote(
                x_ref.at[frames, 192:256],
                xpad.at[frames, 0:64],
                row_send.at[pair, 0],
                row_recv.at[pair, 0],
                below,
            ),
            remote(
                x_ref.at[frames, 0:64],
                xpad.at[frames, 320:384],
                row_send.at[pair, 1],
                row_recv.at[pair, 1],
                above,
            ),
        ]

    column = lax.broadcasted_iota(jnp.int32, (64, 256), 0)

    def activate(place):
        def body(i, carry):
            frame, row = place(i)
            start = pl.multiple_of(i * 64, 64)
            to = pl.multiple_of(row * 64, 64)
            for half in range(2):
                lanes = slice(half * 256, half * 256 + 256)
                left = pltpu.roll(ybuf[0, pl.ds(start, 64), lanes], 1, 0)
                mid = ybuf[1, pl.ds(start, 64), lanes]
                right = pltpu.roll(ybuf[2, pl.ds(start, 64), lanes], 63, 0)
                v = mid + jnp.where(column == 0, 0.0, left) + jnp.where(column == 63, 0.0, right)
                ext[frame + 2, pl.ds(to, 64), lanes] = (v / (1.0 + jnp.exp(-v))).astype(BF16)
            return carry

        lax.fori_loop(0, 4, body, 0)

    def middle(first, weights=()):
        for dj in range(3):
            for load in weights[3 * dj : 3 * dj + 3]:
                load.wait()
            lhs = jnp.concatenate(
                [
                    xpad[first : first + 2, 64 * (1 + di) : 64 * (1 + di) + 128, :].reshape(256, CH)
                    for di in range(3)
                ],
                axis=1,
            )
            ybuf[dj] = jnp.dot(lhs, w2[dj], preferred_element_type=F32)
        activate(lambda i: (first + i // 2, 1 + i % 2))

    def edges(first):
        @pl.when(s > 0)
        def _():
            rows_in[first][0].wait_recv()

        @pl.when(s < 15)
        def _():
            rows_in[first][1].wait_recv()

        @pl.when(s == 0)
        def _():
            xpad[first : first + 2, 0:64, :] = jnp.zeros((2, 64, CH), BF16)

        @pl.when(s == 15)
        def _():
            xpad[first : first + 2, 320:384, :] = jnp.zeros((2, 64, CH), BF16)

        for dj in range(3):
            lhs = jnp.concatenate(
                [
                    jnp.concatenate(
                        [
                            xpad[first : first + 2, 64 * di : 64 * di + 64, :],
                            xpad[first : first + 2, 64 * (3 + di) : 64 * (3 + di) + 64, :],
                        ],
                        axis=1,
                    ).reshape(256, CH)
                    for di in range(3)
                ],
                axis=1,
            )
            ybuf[dj] = jnp.dot(lhs, w2[dj], preferred_element_type=F32)
        activate(lambda i: (first + i // 2, 3 * (i % 2)))

    later = [
        remote(
            ext.at[4:6, rows],
            ext.at[0:2, rows],
            time_send.at[i],
            time_recv.at[i],
            {"tm": (t + 1) % 8},
        )
        for i, rows in enumerate((slice(64, 192), slice(0, 64), slice(192, 256)))
    ]

    pl.semaphore_wait(barrier, 13)
    @pl.when(s < 15)
    def _():
        rows_in[2][0].start()
        rows_in[0][0].start()

    @pl.when(s > 0)
    def _():
        rows_in[2][1].start()
        rows_in[0][1].start()

    own_x.wait()
    def send_later(pieces):
        @pl.when(t < 7)
        def _():
            for copy in pieces:
                copy.start()

    middle(2, w_loads)
    send_later(later[:1])
    for load in loads:
        load.start()
    edges(2)
    send_later(later[1:])
    middle(0)
    edges(0)

    loads[1].wait()

    def hidden(first):
        lhs = jnp.concatenate(
            [ext[first + 2 - k : first + 4 - k].reshape(512, CH) for k in range(3)], axis=1
        )
        temporal = jnp.dot(lhs, wt[...], preferred_element_type=F32)
        value = xpad[first : first + 2, 64:320, :].reshape(512, CH).astype(F32) + temporal
        value = value.astype(BF16)
        for f in range(2):
            hid[:, :, first + f] = value[256 * f : 256 * f + 256].reshape(8, 2, 16, CH)

    def hid_copies(first, g):
        pair = first // 2
        copies = []
        for o in range(1, 8):
            copies.append(
                remote(
                    hid.at[(t + o) % 8, g, first : first + 2],
                    hall.at[g, t, first : first + 2],
                    hid_send.at[pair, g, o - 1],
                    hid_recv.at[pair, g, o - 1],
                    t_peers[o - 1],
                )
            )
        own = pltpu.make_async_copy(
            hid.at[t, g, first : first + 2], hall.at[g, t, first : first + 2], hid_own.at[pair, g]
        )
        return copies, own

    hid_late = [hid_copies(2, g) for g in range(2)]
    hid_early = [hid_copies(0, g) for g in range(2)]

    def send_hidden(exchange):
        copies, own = exchange
        for copy in copies:
            copy.start()
        own.start()

    hidden(2)
    send_hidden(hid_late[0])

    loads[0].wait()
    for i in range(4):
        cot_t[:, 256 * i : 256 * i + 256] = cot[256 * i : 256 * i + 256, :].T

    def tap(k):
        shifted = ext[2 - k : 6 - k].reshape(1024, CH)
        grad = jnp.dot(cot_t[...], shifted, preferred_element_type=F32).astype(BF16)
        part[:, :, :, k * CH : (k + 1) * CH] = grad.reshape(8, 2, 32, CH)

    tap(0)
    stage1 = [
        remote(
            part.at[:, 1 - core, :, lanes],
            a1.at[:, :, lanes],
            s1_send.at[i],
            s1_recv.at[i],
            core_peer,
        )
        for i, lanes in enumerate((slice(0, CH), slice(CH, TAPS)))
    ]
    stage1[0].start()
    stage2 = []

    def reduce_pair(i):
        lanes = (slice(0, CH), slice(CH, TAPS))[i]
        stage1[i].wait()
        for row in range(8):
            mine = part[row, core, :, lanes].astype(F32)
            r1[row // 4, row % 4, :, lanes] = (mine + a1[row, :, lanes].astype(F32)).astype(BF16)
        for o in range(1, 4):
            copy = remote(
                r1.at[:, (z + o) % 4, :, lanes],
                a2.at[o - 1, :, :, lanes],
                s2_send.at[i, o - 1],
                s2_recv.at[i, o - 1],
                z_peers[o - 1],
            )
            copy.start()
            stage2.append(copy)

    reduce_pair(0)

    @pl.when(t > 0)
    def _():
        for copy in later:
            copy.wait_recv()

    @pl.when(t == 0)
    def _():
        ext[0:2] = jnp.zeros((2, 256, CH), BF16)

    hidden(0)
    send_hidden(hid_early[0])
    send_hidden(hid_late[1])
    send_hidden(hid_early[1])

    tap(1)
    tap(2)
    stage1[1].start()
    scale = 1.0 / (CH**0.5)

    for load in loads[2:]:
        load.wait()

    def project(started, first, g):
        copies, own = started[g]
        for copy in copies:
            copy.wait_recv()
        own.wait()

        def norm_rows(i, carry):
            wide = hall[g, pl.ds(i * 4, 4), first : first + 2].reshape(128, CH).astype(F32)
            inv = 1.0 / jnp.sqrt(jnp.mean(wide * wide, axis=1, keepdims=True) + 1e-06)
            rows = pl.ds(pl.multiple_of(i * 128, 128), 128)
            nrm[rows, :] = (wide * inv * gain_ref[...]).astype(BF16)
            return carry

        lax.fori_loop(0, 2, norm_rows, 0)
        for weight, out in ((wq, qb), (wk, kb), (wv, vb)):
            value = jnp.dot(nrm[...], weight[...], preferred_element_type=F32).astype(BF16)
            out[g, :, first : first + 2] = value.reshape(8, 2, 16, CH)

    def attend(g, tile):
        keys = 256 * (tile + 1)
        base = 256 * tile
        sbuf[:, :keys] = lax.dot_general(
            qb[g, 4 * tile : 4 * tile + 4].reshape(256, CH),
            kb[g, : 4 * tile + 4].reshape(keys, CH),
            (((1,), (1,)), ((), ())),
            preferred_element_type=F32,
        )

        def soft(i, carry):
            rows = pl.ds(pl.multiple_of(i * 64, 64), 64)
            scores = sbuf[rows, :keys] * scale
            row = lax.broadcasted_iota(jnp.int32, (64, keys), 0) + (base + i * 64)
            col = lax.broadcasted_iota(jnp.int32, (64, keys), 1)
            allowed = (((row ^ col) & 15) == 0) & (col <= row)
            scores = jnp.where(allowed, scores, -1e30)
            expon = jnp.where(
                allowed, jnp.exp(scores - jnp.max(scores, axis=1, keepdims=True)), 0.0
            )
            total = jnp.sum(expon, axis=1, keepdims=True)
            pbuf[rows, :keys] = (expon * (1.0 / total)).astype(BF16)
            return carry

        lax.fori_loop(0, 4, soft, 0)
        values = vb[g, : 4 * tile + 4].reshape(keys, CH)
        ab[...] = jnp.dot(pbuf[:, :keys], values, preferred_element_type=F32).astype(BF16)
        back = jnp.dot(ab[...], wo[...], preferred_element_type=F32)
        frames = slice(16 * tile, 16 * tile + 16)
        wide = hall[g, 4 * tile : 4 * tile + 4].reshape(256, CH).astype(F32)
        enc[g, frames] = (wide + back).astype(BF16).reshape(16, 16, CH)

    def enc_copy(g, o):
        p = (t + o) % 8
        return remote(
            enc.at[g, pl.ds(p * 4, 4)],
            enc_ref.at[:, t, g],
            enc_send.at[g, o],
            enc_recv.at[g, o],
            {"tm": p},
        )

    def enc_local(g):
        return pltpu.make_async_copy(
            enc.at[g, pl.ds(t * 4, 4)], enc_ref.at[:, t, g], enc_own.at[g]
        )

    def send_encoded(g, tile):
        for o in range(8):
            p = (t + o) % 8

            @pl.when(p // 4 == tile)
            def _():
                if o == 0:
                    enc_local(g).start()
                else:
                    enc_copy(g, o).start()

    project(hid_late, 2, 0)
    reduce_pair(1)

    project(hid_early, 0, 0)
    attend(0, 0)
    send_encoded(0, 0)
    attend(0, 1)
    send_encoded(0, 1)
    for copy in stage2:
        copy.wait()
    for i in range(2):
        r2[i] = (
            r1[i, z].astype(F32)
            + a2[0, i].astype(F32)
            + a2[1, i].astype(F32)
            + a2[2, i].astype(F32)
        ).astype(BF16)
    stage3 = remote(r2.at[1 - y], a3, s3_send.at[0], s3_recv.at[0], y_peer)
    stage3.start()
    project(hid_late, 2, 1)
    project(hid_early, 0, 1)
    attend(1, 0)
    send_encoded(1, 0)
    attend(1, 1)
    send_encoded(1, 1)
    stage3.wait()
    for k in range(3):
        for q in range(4):
            lanes = slice(k * CH + q * 128, k * CH + q * 128 + 128)
            b4[q, k] = (r2[y, :, lanes].astype(F32) + a3[:, lanes].astype(F32)).astype(BF16)
    stage4 = [
        remote(
            b4.at[((t + o) % 8) // 2],
            a4.at[o - 1],
            s4_send.at[o - 1],
            s4_recv.at[o - 1],
            t_peers[o - 1],
        )
        for o in range(1, 8)
    ]
    for copy in stage4:
        copy.start()

    for copy in stage4:
        copy.wait()
    for k in range(3):
        total = b4[t // 2, k].astype(F32)
        for o in range(7):
            total = total + a4[o, k].astype(F32)
        kg_ref[k] = jnp.where(t % 2 == 0, total[:, :64], total[:, 64:])

    @pl.when(s < 15)
    def _():
        rows_in[2][0].wait_send()
        rows_in[0][0].wait_send()

    @pl.when(s > 0)
    def _():
        rows_in[2][1].wait_send()
        rows_in[0][1].wait_send()

    @pl.when(t < 7)
    def _():
        for copy in later:
            copy.wait_send()

    for started in hid_late + hid_early:
        for copy in started[0]:
            copy.wait_send()
    for g in range(2):
        enc_local(g).wait()
        for o in range(1, 8):
            enc_copy(g, o).wait()


def place(enc_ref, kg_ref, enc_out, kg_out, held, held_grad, in_sem, out_sem):
    pieces = [(enc_ref.at[f], held.at[f], enc_out.at[f]) for f in range(4)]
    pieces.append((kg_ref, held_grad, kg_out))
    loads = [pltpu.make_async_copy(a, b, in_sem.at[i]) for i, (a, b, _) in enumerate(pieces)]
    stores = [pltpu.make_async_copy(b, c, out_sem.at[i]) for i, (_, b, c) in enumerate(pieces)]
    for load in loads:
        load.start()
    for load, store in zip(loads, stores):
        load.wait()
        store.start()
    for store in stores:
        store.wait()


def on_device(
    frames_in,
    spatial_kernel,
    temporal_kernel,
    norm_gain,
    query_weight,
    key_weight,
    value_weight,
    out_weight,
    cotangent,
):
    frames, rows, cols, chans = frames_in.shape
    anywhere = pl.BlockSpec(memory_space=pl.ANY)
    vmem = pl.BlockSpec(memory_space=pltpu.VMEM)
    dma = pltpu.SemaphoreType.DMA
    square = pltpu.VMEM((CH, CH), BF16)
    encoded, grad = pl.pallas_call(
        kernel,
        name="block",
        out_shape=(
            jax.ShapeDtypeStruct((4, 8, 2, 16, CH), BF16),
            jax.ShapeDtypeStruct((3, 32, 64), F32),
        ),
        in_specs=[anywhere] * 3 + [vmem] + [anywhere] * 5,
        out_specs=(anywhere, vmem),
        scratch_shapes=[
            pltpu.VMEM((4, 384, CH), BF16),
            pltpu.VMEM((3, TAPS, CH), BF16),
            pltpu.VMEM((TAPS, CH), BF16),
            square,
            square,
            square,
            square,
            pltpu.VMEM((1024, CH), BF16),
            pltpu.VMEM((CH, 1024), BF16),
            pltpu.VMEM((6, 256, CH), BF16),
            pltpu.VMEM((3, 256, CH), F32),
            pltpu.VMEM((8, 2, 4, 16, CH), BF16),
            pltpu.VMEM((2, 8, 4, 16, CH), BF16),
            pltpu.VMEM((256, CH), BF16),
            pltpu.VMEM((2, 8, 4, 16, CH), BF16),
            pltpu.VMEM((2, 8, 4, 16, CH), BF16),
            pltpu.VMEM((2, 8, 4, 16, CH), BF16),
            pltpu.VMEM((256, 512), F32),
            pltpu.VMEM((256, 512), BF16),
            pltpu.VMEM((256, CH), BF16),
            pltpu.VMEM((2, 32, 16, CH), BF16),
            pltpu.VMEM((8, 2, 32, TAPS), BF16),
            pltpu.VMEM((8, 32, TAPS), BF16),
            pltpu.VMEM((2, 4, 32, TAPS), BF16),
            pltpu.VMEM((3, 2, 32, TAPS), BF16),
            pltpu.VMEM((2, 32, TAPS), BF16),
            pltpu.VMEM((32, TAPS), BF16),
            pltpu.VMEM((4, 3, 32, 128), BF16),
            pltpu.VMEM((7, 3, 32, 128), BF16),
            dma((9,)),
            dma((7,)),
            dma((2, 2)),
            dma((2, 2)),
            dma((3,)),
            dma((3,)),
            dma((2, 2, 7)),
            dma((2, 2, 7)),
            dma((2, 2)),
            dma((2, 8)),
            dma((2, 8)),
            dma((2,)),
            dma((2,)),
            dma((2,)),
            dma((2, 3)),
            dma((2, 3)),
            dma((1,)),
            dma((1,)),
            dma((7,)),
            dma((7,)),
        ],
        compiler_params=pltpu.CompilerParams(
            collective_id=0, has_side_effects=True, vmem_limit_bytes=60 * 1024 * 1024
        ),
    )(
        frames_in.reshape(frames, rows * cols, chans),
        spatial_kernel,
        temporal_kernel.reshape(3 * chans, chans),
        norm_gain.reshape(1, chans),
        query_weight,
        key_weight,
        value_weight,
        out_weight,
        cotangent.reshape(-1, chans),
    )
    encoded, grad = pl.pallas_call(
        place,
        name="place",
        out_shape=(
            jax.ShapeDtypeStruct((frames, rows * cols, chans), BF16),
            jax.ShapeDtypeStruct((3, 32, 64), F32),
        ),
        in_specs=[anywhere] * 2,
        out_specs=(anywhere, anywhere),
        scratch_shapes=[
            pltpu.VMEM((4, 256, CH), BF16),
            pltpu.VMEM((3, 32, 64), F32),
            dma((5,)),
            dma((5,)),
        ],
        compiler_params=pltpu.CompilerParams(vmem_limit_bytes=60 * 1024 * 1024),
    )(encoded.reshape(frames, rows * cols, chans), grad)
    return (encoded.reshape(frames, rows, cols, chans), grad.transpose(0, 2, 1))


def solution(mesh):
    tile = P("tm", "space", None, None)
    in_specs = (tile, P(), P(), P(), P(), P(), P(), P(), tile)
    out_specs = (tile, P(None, "tm", "space"))
    return jax.shard_map(
        on_device, mesh=mesh, in_specs=in_specs, out_specs=out_specs, check_vma=False
    )
```

```python
import functools

import jax
import jax.numpy as jnp
from jax import lax
from jax.experimental import pallas as pl
from jax.experimental.pallas import tpu as pltpu
from jax.sharding import PartitionSpec as P

F32 = jnp.float32
BF16 = jnp.bfloat16
MESH = pl.DeviceIdType.MESH
CH = 512
TAPS = 3 * CH


def remote(src, dst, send_sem, recv_sem, device):
    return pltpu.make_async_remote_copy(
        src_ref=src,
        dst_ref=dst,
        send_sem=send_sem,
        recv_sem=recv_sem,
        device_id=device,
        device_id_type=MESH,
    )


def kernel(
    x_ref,
    wsp_ref,
    wt_ref,
    gain_ref,
    wq_ref,
    wk_ref,
    wv_ref,
    wo_ref,
    cot_ref,
    enc_ref,
    kg_ref,
    xpad,
    w2,
    wt,
    wq,
    wk,
    wv,
    wo,
    cot,
    cot_t,
    ext,
    ybuf,
    hid,
    hall,
    nrm,
    qb,
    kb,
    vb,
    sbuf,
    pbuf,
    ab,
    enc,
    part,
    a1,
    r1,
    a2,
    r2,
    a3,
    b4,
    a4,
    w_sem,
    l_sem,
    row_send,
    row_recv,
    time_send,
    time_recv,
    hid_send,
    hid_recv,
    hid_own,
    enc_send,
    enc_recv,
    enc_own,
    s1_send,
    s1_recv,
    s2_send,
    s2_recv,
    s3_send,
    s3_recv,
    s4_send,
    s4_recv,
):
    t = lax.axis_index("tm")
    s = lax.axis_index("space")
    core = s % 2
    z = (s // 2) % 4
    y = s // 8

    below = {"space": (s + 1) % 16}
    above = {"space": (s + 15) % 16}
    z_peers = [{"space": y * 8 + ((z + o) % 4) * 2 + core} for o in range(1, 4)]
    y_peer = {"space": (1 - y) * 8 + z * 2 + core}
    core_peer = {"space": s + 1 - 2 * core}
    t_peers = [{"tm": (t + o) % 8} for o in range(1, 8)]

    barrier = pltpu.get_barrier_semaphore()
    for peer in [below, above, y_peer] + z_peers + t_peers:
        pl.semaphore_signal(barrier, inc=1, device_id=peer, device_id_type=MESH)

    own_x = pltpu.make_async_copy(x_ref, xpad.at[:, 64:320], l_sem.at[0])
    own_x.start()
    w_loads = []
    for dj in range(3):
        for di in range(3):
            load = pltpu.make_async_copy(
                wsp_ref.at[di, dj], w2.at[dj, di * CH : (di + 1) * CH], w_sem.at[3 * dj + di]
            )
            load.start()
            w_loads.append(load)
    loads = []
    for i, (src, dst) in enumerate(
        ((cot_ref, cot), (wt_ref, wt), (wq_ref, wq), (wk_ref, wk), (wv_ref, wv), (wo_ref, wo))
    ):
        loads.append(pltpu.make_async_copy(src, dst, l_sem.at[1 + i]))

    rows_in = {}
    for first in (2, 0):
        frames = slice(first, first + 2)
        pair = first // 2
        rows_in[first] = [
            remote(
                x_ref.at[frames, 192:256],
                xpad.at[frames, 0:64],
                row_send.at[pair, 0],
                row_recv.at[pair, 0],
                below,
            ),
            remote(
                x_ref.at[frames, 0:64],
                xpad.at[frames, 320:384],
                row_send.at[pair, 1],
                row_recv.at[pair, 1],
                above,
            ),
        ]

    column = lax.broadcasted_iota(jnp.int32, (64, 256), 0)

    def activate(place):
        def body(i, carry):
            frame, row = place(i)
            start = pl.multiple_of(i * 64, 64)
            to = pl.multiple_of(row * 64, 64)
            for half in range(2):
                lanes = slice(half * 256, half * 256 + 256)
                left = pltpu.roll(ybuf[0, pl.ds(start, 64), lanes], 1, 0)
                mid = ybuf[1, pl.ds(start, 64), lanes]
                right = pltpu.roll(ybuf[2, pl.ds(start, 64), lanes], 63, 0)
                v = mid + jnp.where(column == 0, 0.0, left) + jnp.where(column == 63, 0.0, right)
                ext[frame + 2, pl.ds(to, 64), lanes] = (v / (1.0 + jnp.exp(-v))).astype(BF16)
            return carry

        lax.fori_loop(0, 4, body, 0)

    def middle(first, weights=()):
        for dj in range(3):
            for load in weights[3 * dj : 3 * dj + 3]:
                load.wait()
            lhs = jnp.concatenate(
                [
                    xpad[first : first + 2, 64 * (1 + di) : 64 * (1 + di) + 128, :].reshape(256, CH)
                    for di in range(3)
                ],
                axis=1,
            )
            ybuf[dj] = jnp.dot(lhs, w2[dj], preferred_element_type=F32)
        activate(lambda i: (first + i // 2, 1 + i % 2))

    def edges(first):
        @pl.when(s > 0)
        def _():
            rows_in[first][0].wait_recv()

        @pl.when(s < 15)
        def _():
            rows_in[first][1].wait_recv()

        @pl.when(s == 0)
        def _():
            xpad[first : first + 2, 0:64, :] = jnp.zeros((2, 64, CH), BF16)

        @pl.when(s == 15)
        def _():
            xpad[first : first + 2, 320:384, :] = jnp.zeros((2, 64, CH), BF16)

        for dj in range(3):
            lhs = jnp.concatenate(
                [
                    jnp.concatenate(
                        [
                            xpad[first : first + 2, 64 * di : 64 * di + 64, :],
                            xpad[first : first + 2, 64 * (3 + di) : 64 * (3 + di) + 64, :],
                        ],
                        axis=1,
                    ).reshape(256, CH)
                    for di in range(3)
                ],
                axis=1,
            )
            ybuf[dj] = jnp.dot(lhs, w2[dj], preferred_element_type=F32)
        activate(lambda i: (first + i // 2, 3 * (i % 2)))

    later = [
        remote(
            ext.at[4:6, rows],
            ext.at[0:2, rows],
            time_send.at[i],
            time_recv.at[i],
            {"tm": (t + 1) % 8},
        )
        for i, rows in enumerate((slice(64, 192), slice(0, 64), slice(192, 256)))
    ]

    pl.semaphore_wait(barrier, 13)
    @pl.when(s < 15)
    def _():
        rows_in[2][0].start()
        rows_in[0][0].start()

    @pl.when(s > 0)
    def _():
        rows_in[2][1].start()
        rows_in[0][1].start()

    own_x.wait()
    def send_later(pieces):
        @pl.when(t < 7)
        def _():
            for copy in pieces:
                copy.start()

    middle(2, w_loads)
    send_later(later[:1])
    for load in loads:
        load.start()
    edges(2)
    send_later(later[1:])
    middle(0)
    edges(0)

    loads[1].wait()

    def hidden(first):
        lhs = jnp.concatenate(
            [ext[first + 2 - k : first + 4 - k].reshape(512, CH) for k in range(3)], axis=1
        )
        temporal = jnp.dot(lhs, wt[...], preferred_element_type=F32)
        value = xpad[first : first + 2, 64:320, :].reshape(512, CH).astype(F32) + temporal
        value = value.astype(BF16)
        for f in range(2):
            hid[:, :, first + f] = value[256 * f : 256 * f + 256].reshape(8, 2, 16, CH)

    def hid_copies(first, g):
        pair = first // 2
        copies = []
        for o in range(1, 8):
            copies.append(
                remote(
                    hid.at[(t + o) % 8, g, first : first + 2],
                    hall.at[g, t, first : first + 2],
                    hid_send.at[pair, g, o - 1],
                    hid_recv.at[pair, g, o - 1],
                    t_peers[o - 1],
                )
            )
        own = pltpu.make_async_copy(
            hid.at[t, g, first : first + 2], hall.at[g, t, first : first + 2], hid_own.at[pair, g]
        )
        return copies, own

    hid_late = [hid_copies(2, g) for g in range(2)]
    hid_early = [hid_copies(0, g) for g in range(2)]

    def send_hidden(exchange):
        copies, own = exchange
        for copy in copies:
            copy.start()
        own.start()

    hidden(2)
    send_hidden(hid_late[0])

    loads[0].wait()
    for i in range(4):
        cot_t[:, 256 * i : 256 * i + 256] = cot[256 * i : 256 * i + 256, :].T

    def tap(k):
        shifted = ext[2 - k : 6 - k].reshape(1024, CH)
        grad = jnp.dot(cot_t[...], shifted, preferred_element_type=F32).astype(BF16)
        part[:, :, :, k * CH : (k + 1) * CH] = grad.reshape(8, 2, 32, CH)

    tap(0)
    stage1 = [
        remote(
            part.at[:, 1 - core, :, lanes],
            a1.at[:, :, lanes],
            s1_send.at[i],
            s1_recv.at[i],
            core_peer,
        )
        for i, lanes in enumerate((slice(0, CH), slice(CH, TAPS)))
    ]
    stage1[0].start()
    stage2 = []

    def reduce_pair(i):
        lanes = (slice(0, CH), slice(CH, TAPS))[i]
        stage1[i].wait()
        for row in range(8):
            mine = part[row, core, :, lanes].astype(F32)
            r1[row // 4, row % 4, :, lanes] = (mine + a1[row, :, lanes].astype(F32)).astype(BF16)
        for o in range(1, 4):
            copy = remote(
                r1.at[:, (z + o) % 4, :, lanes],
                a2.at[o - 1, :, :, lanes],
                s2_send.at[i, o - 1],
                s2_recv.at[i, o - 1],
                z_peers[o - 1],
            )
            copy.start()
            stage2.append(copy)

    reduce_pair(0)

    @pl.when(t > 0)
    def _():
        for copy in later:
            copy.wait_recv()

    @pl.when(t == 0)
    def _():
        ext[0:2] = jnp.zeros((2, 256, CH), BF16)

    hidden(0)
    send_hidden(hid_early[0])
    send_hidden(hid_late[1])
    send_hidden(hid_early[1])

    tap(1)
    tap(2)
    stage1[1].start()
    scale = 1.0 / (CH**0.5)

    for load in loads[2:]:
        load.wait()

    def project(started, first, g):
        copies, own = started[g]
        for copy in copies:
            copy.wait_recv()
        own.wait()

        def norm_rows(i, carry):
            wide = hall[g, pl.ds(i * 4, 4), first : first + 2].reshape(128, CH).astype(F32)
            inv = 1.0 / jnp.sqrt(jnp.mean(wide * wide, axis=1, keepdims=True) + 1e-06)
            rows = pl.ds(pl.multiple_of(i * 128, 128), 128)
            nrm[rows, :] = (wide * inv * gain_ref[...]).astype(BF16)
            return carry

        lax.fori_loop(0, 2, norm_rows, 0)
        for weight, out in ((wq, qb), (wk, kb), (wv, vb)):
            value = jnp.dot(nrm[...], weight[...], preferred_element_type=F32).astype(BF16)
            out[g, :, first : first + 2] = value.reshape(8, 2, 16, CH)

    def attend(g, tile):
        keys = 256 * (tile + 1)
        base = 256 * tile
        sbuf[:, :keys] = lax.dot_general(
            qb[g, 4 * tile : 4 * tile + 4].reshape(256, CH),
            kb[g, : 4 * tile + 4].reshape(keys, CH),
            (((1,), (1,)), ((), ())),
            preferred_element_type=F32,
        )

        def soft(i, carry):
            rows = pl.ds(pl.multiple_of(i * 64, 64), 64)
            scores = sbuf[rows, :keys] * scale
            row = lax.broadcasted_iota(jnp.int32, (64, keys), 0) + (base + i * 64)
            col = lax.broadcasted_iota(jnp.int32, (64, keys), 1)
            allowed = (((row ^ col) & 15) == 0) & (col <= row)
            scores = jnp.where(allowed, scores, -1e30)
            expon = jnp.where(
                allowed, jnp.exp(scores - jnp.max(scores, axis=1, keepdims=True)), 0.0
            )
            total = jnp.sum(expon, axis=1, keepdims=True)
            pbuf[rows, :keys] = (expon * (1.0 / total)).astype(BF16)
            return carry

        lax.fori_loop(0, 4, soft, 0)
        values = vb[g, : 4 * tile + 4].reshape(keys, CH)
        ab[...] = jnp.dot(pbuf[:, :keys], values, preferred_element_type=F32).astype(BF16)
        back = jnp.dot(ab[...], wo[...], preferred_element_type=F32)
        frames = slice(16 * tile, 16 * tile + 16)
        wide = hall[g, 4 * tile : 4 * tile + 4].reshape(256, CH).astype(F32)
        enc[g, frames] = (wide + back).astype(BF16).reshape(16, 16, CH)

    def enc_copy(g, o):
        p = (t + o) % 8
        return remote(
            enc.at[g, pl.ds(p * 4, 4)],
            enc_ref.at[:, t, g],
            enc_send.at[g, o],
            enc_recv.at[g, o],
            {"tm": p},
        )

    def enc_local(g):
        return pltpu.make_async_copy(
            enc.at[g, pl.ds(t * 4, 4)], enc_ref.at[:, t, g], enc_own.at[g]
        )

    def send_encoded(g, tile):
        for o in range(8):
            p = (t + o) % 8

            @pl.when(p // 4 == tile)
            def _():
                if o == 0:
                    enc_local(g).start()
                else:
                    enc_copy(g, o).start()

    project(hid_late, 2, 0)
    reduce_pair(1)

    project(hid_early, 0, 0)
    attend(0, 0)
    send_encoded(0, 0)
    attend(0, 1)
    send_encoded(0, 1)
    for copy in stage2:
        copy.wait()
    for i in range(2):
        r2[i] = (
            r1[i, z].astype(F32)
            + a2[0, i].astype(F32)
            + a2[1, i].astype(F32)
            + a2[2, i].astype(F32)
        ).astype(BF16)
    stage3 = remote(r2.at[1 - y], a3, s3_send.at[0], s3_recv.at[0], y_peer)
    stage3.start()
    project(hid_late, 2, 1)
    project(hid_early, 0, 1)
    attend(1, 0)
    send_encoded(1, 0)
    attend(1, 1)
    stage3.wait()
    for k in range(3):
        for q in range(4):
            lanes = slice(k * CH + q * 128, k * CH + q * 128 + 128)
            b4[q, k] = (r2[y, :, lanes].astype(F32) + a3[:, lanes].astype(F32)).astype(BF16)
    stage4 = [
        remote(
            b4.at[((t + o) % 8) // 2],
            a4.at[o - 1],
            s4_send.at[o - 1],
            s4_recv.at[o - 1],
            t_peers[o - 1],
        )
        for o in range(1, 8)
    ]
    for copy in stage4:
        copy.start()
    send_encoded(1, 1)

    for copy in stage4:
        copy.wait()
    for k in range(3):
        total = b4[t // 2, k].astype(F32)
        for o in range(7):
            total = total + a4[o, k].astype(F32)
        kg_ref[k] = jnp.where(t % 2 == 0, total[:, :64], total[:, 64:])

    @pl.when(s < 15)
    def _():
        rows_in[2][0].wait_send()
        rows_in[0][0].wait_send()

    @pl.when(s > 0)
    def _():
        rows_in[2][1].wait_send()
        rows_in[0][1].wait_send()

    @pl.when(t < 7)
    def _():
        for copy in later:
            copy.wait_send()

    for started in hid_late + hid_early:
        for copy in started[0]:
            copy.wait_send()
    for g in range(2):
        enc_local(g).wait()
        for o in range(1, 8):
            enc_copy(g, o).wait()


def place(enc_ref, kg_ref, enc_out, kg_out, held, held_grad, in_sem, out_sem):
    pieces = [(enc_ref.at[f], held.at[f], enc_out.at[f]) for f in range(4)]
    pieces.append((kg_ref, held_grad, kg_out))
    loads = [pltpu.make_async_copy(a, b, in_sem.at[i]) for i, (a, b, _) in enumerate(pieces)]
    stores = [pltpu.make_async_copy(b, c, out_sem.at[i]) for i, (_, b, c) in enumerate(pieces)]
    for load in loads:
        load.start()
    for load, store in zip(loads, stores):
        load.wait()
        store.start()
    for store in stores:
        store.wait()


def on_device(
    frames_in,
    spatial_kernel,
    temporal_kernel,
    norm_gain,
    query_weight,
    key_weight,
    value_weight,
    out_weight,
    cotangent,
):
    frames, rows, cols, chans = frames_in.shape
    anywhere = pl.BlockSpec(memory_space=pl.ANY)
    vmem = pl.BlockSpec(memory_space=pltpu.VMEM)
    dma = pltpu.SemaphoreType.DMA
    square = pltpu.VMEM((CH, CH), BF16)
    encoded, grad = pl.pallas_call(
        kernel,
        name="block",
        out_shape=(
            jax.ShapeDtypeStruct((4, 8, 2, 16, CH), BF16),
            jax.ShapeDtypeStruct((3, 32, 64), F32),
        ),
        in_specs=[anywhere] * 3 + [vmem] + [anywhere] * 5,
        out_specs=(anywhere, vmem),
        scratch_shapes=[
            pltpu.VMEM((4, 384, CH), BF16),
            pltpu.VMEM((3, TAPS, CH), BF16),
            pltpu.VMEM((TAPS, CH), BF16),
            square,
            square,
            square,
            square,
            pltpu.VMEM((1024, CH), BF16),
            pltpu.VMEM((CH, 1024), BF16),
            pltpu.VMEM((6, 256, CH), BF16),
            pltpu.VMEM((3, 256, CH), F32),
            pltpu.VMEM((8, 2, 4, 16, CH), BF16),
            pltpu.VMEM((2, 8, 4, 16, CH), BF16),
            pltpu.VMEM((256, CH), BF16),
            pltpu.VMEM((2, 8, 4, 16, CH), BF16),
            pltpu.VMEM((2, 8, 4, 16, CH), BF16),
            pltpu.VMEM((2, 8, 4, 16, CH), BF16),
            pltpu.VMEM((256, 512), F32),
            pltpu.VMEM((256, 512), BF16),
            pltpu.VMEM((256, CH), BF16),
            pltpu.VMEM((2, 32, 16, CH), BF16),
            pltpu.VMEM((8, 2, 32, TAPS), BF16),
            pltpu.VMEM((8, 32, TAPS), BF16),
            pltpu.VMEM((2, 4, 32, TAPS), BF16),
            pltpu.VMEM((3, 2, 32, TAPS), BF16),
            pltpu.VMEM((2, 32, TAPS), BF16),
            pltpu.VMEM((32, TAPS), BF16),
            pltpu.VMEM((4, 3, 32, 128), BF16),
            pltpu.VMEM((7, 3, 32, 128), BF16),
            dma((9,)),
            dma((7,)),
            dma((2, 2)),
            dma((2, 2)),
            dma((3,)),
            dma((3,)),
            dma((2, 2, 7)),
            dma((2, 2, 7)),
            dma((2, 2)),
            dma((2, 8)),
            dma((2, 8)),
            dma((2,)),
            dma((2,)),
            dma((2,)),
            dma((2, 3)),
            dma((2, 3)),
            dma((1,)),
            dma((1,)),
            dma((7,)),
            dma((7,)),
        ],
        compiler_params=pltpu.CompilerParams(
            collective_id=0, has_side_effects=True, vmem_limit_bytes=60 * 1024 * 1024
        ),
    )(
        frames_in.reshape(frames, rows * cols, chans),
        spatial_kernel,
        temporal_kernel.reshape(3 * chans, chans),
        norm_gain.reshape(1, chans),
        query_weight,
        key_weight,
        value_weight,
        out_weight,
        cotangent.reshape(-1, chans),
    )
    encoded, grad = pl.pallas_call(
        place,
        name="place",
        out_shape=(
            jax.ShapeDtypeStruct((frames, rows * cols, chans), BF16),
            jax.ShapeDtypeStruct((3, 32, 64), F32),
        ),
        in_specs=[anywhere] * 2,
        out_specs=(anywhere, anywhere),
        scratch_shapes=[
            pltpu.VMEM((4, 256, CH), BF16),
            pltpu.VMEM((3, 32, 64), F32),
            dma((5,)),
            dma((5,)),
        ],
        compiler_params=pltpu.CompilerParams(vmem_limit_bytes=60 * 1024 * 1024),
    )(encoded.reshape(frames, rows * cols, chans), grad)
    return (encoded.reshape(frames, rows, cols, chans), grad.transpose(0, 2, 1))


def solution(mesh):
    tile = P("tm", "space", None, None)
    in_specs = (tile, P(), P(), P(), P(), P(), P(), P(), tile)
    out_specs = (tile, P(None, "tm", "space"))
    return jax.shard_map(
        on_device, mesh=mesh, in_specs=in_specs, out_specs=out_specs, check_vma=False
    )
```
